1024 devices in a mesh: dp: 32 (over y, x_lo, core), blk: 32 (over z, x_hi).
Axes of the slice: x: 8 (x_hi: 4, x_lo: 2; x = x_hi * 2 + x_lo), y: 8, z: 8, core: 2. Of those that a mesh axis runs over, the one named last changes fastest.
Arguments:
- captions: bfloat16 [16384, 1152], P('dp'), may hold values from -6 to 6
- w_in: bfloat16 [1152, 4096], P(None, 'blk'), may hold values from -0.1875 to 0.1875
- w_out: bfloat16 [4096, 1152], P('blk'), may hold values from -0.09375 to 0.09375
- images: bfloat16 [1024, 1152], P('blk'), may hold values from -6 to 6
- pairs: int32 [16384], P('dp'), may hold values from 0 to 1023
Outputs:
- grad_w_in: float32 [1152, 4096], P('dp', 'blk')
- grad_w_out_t: float32 [1152, 4096], P('dp', 'blk')
The draws below stay inside these ranges and needn't reach their ends.
All inputs are finite; a program needn't handle non-finite values.
Results may differ from the reference program's by a relative error of at most 0.005.
Values may be sent and summed in bfloat16 or wider, within the bound.
No kernel may reach another device: no remote copies, remote signals or barrier semaphores. Data moves between devices by JAX's collectives and lax.ppermute only.
A program may use at most 32 MiB of HBM per device.

```python
import jax
import jax.numpy as jnp
from jax import lax

D = 1152
FF = 4096
CAPS = 16384
IMGS = 1024


def set_ends(entries, stream_key, low, high):
    longest = entries.shape.index(max(entries.shape))
    spots = []
    for shift in (0, 1):
        where = [jax.random.randint(jax.random.fold_in(stream_key, axis), (), 0, length) for axis, length in enumerate(entries.shape)]
        where[longest] = (where[longest] + shift) % entries.shape[longest]
        spots.append(tuple(where))
    return entries.at[spots[0]].set(low).at[spots[1]].set(high)


def block_levels(rng, extent, cuts, smallest, high):
    loudness, own = 1.0, jax.random.fold_in(rng, 6)
    for dim, parts in cuts:
        draws = jnp.exp(jax.random.uniform(jax.random.fold_in(own, dim), (parts,), jnp.float32, smallest / len(cuts), high / len(cuts)))
        loudness = loudness * jnp.repeat(draws, extent[dim] // parts).reshape([-1 if axis == dim else 1 for axis in range(len(extent))])
    return loudness


def normal_values(stream_key, shape, scale, limit, pieces=(), held_as=jnp.bfloat16):
    drawn = jax.random.normal(stream_key, shape, jnp.float32) * scale
    if len(pieces) > 0:
        drawn = block_levels(stream_key, shape, pieces, -0.22, 0.18) * drawn
    return jnp.clip(drawn, min=-limit, max=limit).astype(held_as)


def setup_inputs(seed: int = 0) -> dict:
    arg_keys = jax.random.split(jax.random.key(seed), 6)
    captions = normal_values(arg_keys[0], (CAPS, D), 1.0, 6.0, ((0, 32),))
    w_in = normal_values(arg_keys[1], (D, FF), D ** -0.5, 0.1875, ((1, 32),))
    w_out = normal_values(arg_keys[2], (FF, D), FF ** -0.5, 0.09375, ((0, 32),))
    images = normal_values(arg_keys[3], (IMGS, D), 1.0, 6.0, ((0, 32),))
    pairs = set_ends(jax.random.randint(arg_keys[4], (CAPS,), 0, IMGS), jax.random.fold_in(arg_keys[4], 1), 0, IMGS - 1).astype(jnp.int32)
    return {"captions": captions, "w_in": w_in, "w_out": w_out, "images": images, "pairs": pairs}


SCORE_SCALE = 10.0
SCORE_BIAS_TERM = -5.0
EPSILON = 1e-06

def activate(values):
    return jax.nn.gelu(values, approximate=True)

def reference(captions, w_in, w_out, images, pairs):
    pre_act = jnp.dot(captions, w_in, preferred_element_type=jnp.float32)
    hidden = activate(pre_act).astype(jnp.bfloat16)
    embedding = jnp.dot(hidden, w_out, preferred_element_type=jnp.float32)
    inv_norm = lax.rsqrt(lax.optimization_barrier(jnp.sum(embedding * embedding, axis=1, keepdims=True)) + EPSILON)
    unit_dir = embedding * inv_norm
    direction_halfway = unit_dir.astype(jnp.bfloat16)
    image_vals = images.astype(jnp.float32)
    image_direction = (image_vals * lax.rsqrt(lax.optimization_barrier(jnp.sum(image_vals * image_vals, axis=1, keepdims=True)) + EPSILON)).astype(jnp.bfloat16)
    pair_scores = SCORE_SCALE * jnp.dot(direction_halfway, image_direction.T, preferred_element_type=jnp.float32) + SCORE_BIAS_TERM
    columns = jnp.arange(IMGS, dtype=jnp.int32)
    labels = (pairs[:, None] == columns[None, :]).astype(jnp.float32)
    label_error = (jax.nn.sigmoid(pair_scores) - labels).astype(jnp.bfloat16)
    direction_gradient = SCORE_SCALE * jnp.dot(label_error, image_direction, preferred_element_type=jnp.float32)
    embed_grad = (direction_gradient - unit_dir * lax.optimization_barrier(jnp.sum(unit_dir * direction_gradient, axis=1, keepdims=True))) * inv_norm
    embed_half = embed_grad.astype(jnp.bfloat16)
    hidden_grad = jnp.dot(embed_half, w_out.T, preferred_element_type=jnp.float32)
    _, pullback = jax.vjp(activate, pre_act)
    preact_grad = pullback(hidden_grad)[0].astype(jnp.bfloat16)
    grad_w_in = jnp.dot(captions.T, preact_grad, preferred_element_type=jnp.float32)
    grad_w_out_t = jnp.dot(embed_half.T, hidden, preferred_element_type=jnp.float32)
    return (grad_w_in, grad_w_out_t)
```

```python
import jax
import jax.numpy as jnp
from jax import lax
from jax.sharding import Mesh
from jax.sharding import PartitionSpec as P

DP = ("y", "xl", "core")
BLK = ("z", "xh")
PAIR = ("xl", "core")

SCALE = 10.0
BIAS = -5.0
EPS = 1e-06
BF16 = jnp.bfloat16
F32 = jnp.float32


def exchange(x, axes):
    return lax.all_to_all(x, axes, 0, 0, tiled=True)


def to_all(x, n):
    return jnp.broadcast_to(x[None], (n, *x.shape))


def activate(values):
    return jax.nn.gelu(values, approximate=True)


def body(captions, w_in, w_out, images, pairs):
    rows, width = captions.shape
    n_z, n_xh, n_y = lax.axis_size("z"), lax.axis_size("xh"), lax.axis_size("y")
    n_c = lax.axis_size("xl") * lax.axis_size("core")
    n_dp = n_y * n_c
    per_xh = rows // n_xh
    own = per_xh // n_z
    img_block = images.shape[0]
    img_part = img_block // n_c
    c = lax.axis_index(PAIR)

    img = lax.dynamic_slice_in_dim(images, c * img_part, img_part, 0).astype(F32)
    img = (img * lax.rsqrt(jnp.sum(img * img, axis=1, keepdims=True) + EPS)).astype(BF16)

    pre_act = jnp.dot(captions, w_in, preferred_element_type=F32)
    hidden = activate(pre_act).astype(BF16)
    partial = jnp.dot(hidden, w_out, preferred_element_type=F32).astype(BF16)

    sent = jnp.concatenate([partial.reshape(n_xh, per_xh, width), to_all(img, n_xh)], axis=1)
    got = exchange(sent, "xh")
    partial = jnp.sum(got[:, :per_xh].astype(F32), axis=0).astype(BF16)
    img = got[:, per_xh:].reshape(n_xh * img_part, width)
    sent = jnp.concatenate([partial.reshape(n_z, own, width), to_all(img, n_z)], axis=1)
    got = exchange(sent, "z")
    embedding = jnp.sum(got[:, :own].astype(F32), axis=0)
    img = got[:, own:].reshape(-1, width)
    n_img = img.shape[0]

    inv_norm = lax.rsqrt(jnp.sum(embedding * embedding, axis=1, keepdims=True) + EPS)
    unit_dir = embedding * inv_norm

    first = lax.axis_index("xh") * per_xh + lax.axis_index("z") * own
    pair = lax.dynamic_slice_in_dim(pairs, first, own, 0)[:, None]
    lane = lax.broadcasted_iota(jnp.int32, (own, 128), 1)
    digits = jnp.where(lane == 0, pair // 32, jnp.where(lane == 1, pair % 32, 0)).astype(BF16)
    got = exchange(to_all(jnp.concatenate([unit_dir.astype(BF16), digits], axis=1), n_c), PAIR)
    got = got.reshape(n_c * own, width + 128)
    unit_half = got[:, :width]
    pair = (got[:, width : width + 1].astype(F32) * 32 + got[:, width + 1 : width + 2].astype(F32)).astype(jnp.int32)

    logits = (
        SCALE * lax.dot_general(unit_half, img, (((1,), (1,)), ((), ())), preferred_element_type=F32) + BIAS
    )
    n = lax.broadcasted_iota(jnp.int32, (1, n_img), 1)
    column = (n // img_part) * img_block + c * img_part + n % img_part
    label = (pair == column).astype(F32)
    mismatch = (jax.nn.sigmoid(logits) - label).astype(BF16)
    grad = SCALE * jnp.dot(mismatch, img, preferred_element_type=F32)
    unit_grad = jnp.sum(exchange(grad.reshape(n_c, own, width), PAIR), axis=0)

    embed_half = (
        (unit_grad - unit_dir * jnp.sum(unit_dir * unit_grad, axis=1, keepdims=True)) * inv_norm
    ).astype(BF16)
    got = exchange(to_all(embed_half, n_z), "z").reshape(per_xh, width)
    embed_half = exchange(to_all(got, n_xh), "xh").reshape(rows, width)

    hidden_grad = lax.dot_general(embed_half, w_out, (((1,), (1,)), ((), ())), preferred_element_type=F32)
    _, pullback = jax.vjp(activate, pre_act)
    preact_grad = pullback(hidden_grad)[0].astype(BF16)
    grad_in = lax.dot_general(captions, preact_grad, (((0,), (0,)), ((), ())), preferred_element_type=F32)
    grad_out = lax.dot_general(embed_half, hidden, (((0,), (0,)), ((), ())), preferred_element_type=F32)
    share = width // n_dp
    sent = jnp.concatenate(
        [grad_in.astype(BF16).reshape(n_dp, share, -1), grad_out.astype(BF16).reshape(n_dp, share, -1)], axis=1
    )
    total = jnp.sum(exchange(sent, DP).astype(F32), axis=0)
    return total[:share], total[share:]


def solution(mesh):
    fine = Mesh(mesh.devices.reshape(8, 2, 2, 8, 4), (*DP, *BLK))
    placed = (P(DP, None), P(None, BLK), P(BLK, None), P(BLK, None), P(DP))
    return jax.shard_map(
        body, mesh=fine, in_specs=placed, out_specs=(P(DP, BLK), P(DP, BLK)), check_vma=False
    )
```

```python
import jax
import jax.numpy as jnp
from jax import lax
from jax.sharding import Mesh
from jax.sharding import PartitionSpec as P

DP = ("y", "xl", "core")
BLK = ("z", "xh")
PAIR = ("xl", "core")

SCALE = 10.0
BIAS = -5.0
EPS = 1e-06
BF16 = jnp.bfloat16
F32 = jnp.float32


def exchange(x, axes):
    return lax.all_to_all(x, axes, 0, 0, tiled=True)


def to_all(x, n):
    return jnp.broadcast_to(x[None], (n, *x.shape))


def activate(values):
    return jax.nn.gelu(values, approximate=True)


def body(captions, w_in, w_out, images, pairs):
    rows, width = captions.shape
    n_blk, n_dp, n_c = lax.axis_size(BLK), lax.axis_size(DP), lax.axis_size(PAIR)
    own = rows // n_blk
    img_block = images.shape[0]
    img_part = img_block // n_c
    c = lax.axis_index(PAIR)

    img = lax.dynamic_slice_in_dim(images, c * img_part, img_part, 0).astype(F32)
    img = (img * lax.rsqrt(jnp.sum(img * img, axis=1, keepdims=True) + EPS)).astype(BF16)

    pre_act = jnp.dot(captions, w_in, preferred_element_type=F32)
    hidden = activate(pre_act).astype(BF16)
    partial = jnp.dot(hidden, w_out, preferred_element_type=F32).astype(BF16)

    sent = jnp.concatenate([partial.reshape(n_blk, own, width), to_all(img, n_blk)], axis=1)
    got = exchange(sent, BLK)
    embedding = jnp.sum(got[:, :own].astype(F32), axis=0)
    img = got[:, own:].reshape(-1, width)
    n_img = img.shape[0]

    inv_norm = lax.rsqrt(jnp.sum(embedding * embedding, axis=1, keepdims=True) + EPS)
    unit_dir = embedding * inv_norm

    pair = lax.dynamic_slice_in_dim(pairs, lax.axis_index(BLK) * own, own, 0)[:, None]
    lane = lax.broadcasted_iota(jnp.int32, (own, 128), 1)
    digits = jnp.where(lane == 0, pair // 32, jnp.where(lane == 1, pair % 32, 0)).astype(BF16)
    got = exchange(to_all(jnp.concatenate([unit_dir.astype(BF16), digits], axis=1), n_c), PAIR)
    got = got.reshape(n_c * own, width + 128)
    unit_half = got[:, :width]
    pair = (got[:, width : width + 1].astype(F32) * 32 + got[:, width + 1 : width + 2].astype(F32)).astype(jnp.int32)

    logits = (
        SCALE * lax.dot_general(unit_half, img, (((1,), (1,)), ((), ())), preferred_element_type=F32) + BIAS
    )
    n = lax.broadcasted_iota(jnp.int32, (1, n_img), 1)
    column = (n // img_part) * img_block + c * img_part + n % img_part
    label = (pair == column).astype(F32)
    mismatch = (jax.nn.sigmoid(logits) - label).astype(BF16)
    grad = SCALE * jnp.dot(mismatch, img, preferred_element_type=F32)
    unit_grad = jnp.sum(exchange(grad.reshape(n_c, own, width), PAIR), axis=0)

    embed_half = (
        (unit_grad - unit_dir * jnp.sum(unit_dir * unit_grad, axis=1, keepdims=True)) * inv_norm
    ).astype(BF16)
    embed_half = exchange(to_all(embed_half, n_blk), BLK).reshape(rows, width)

    hidden_grad = lax.dot_general(embed_half, w_out, (((1,), (1,)), ((), ())), preferred_element_type=F32)
    _, pullback = jax.vjp(activate, pre_act)
    preact_grad = pullback(hidden_grad)[0].astype(BF16)
    grad_in = lax.dot_general(captions, preact_grad, (((0,), (0,)), ((), ())), preferred_element_type=F32)
    grad_out = lax.dot_general(embed_half, hidden, (((0,), (0,)), ((), ())), preferred_element_type=F32)
    share = width // n_dp
    sent = jnp.concatenate(
        [grad_in.astype(BF16).reshape(n_dp, share, -1), grad_out.astype(BF16).reshape(n_dp, share, -1)], axis=1
    )
    total = jnp.sum(exchange(sent, DP).astype(F32), axis=0)
    return total[:share], total[share:]


def solution(mesh):
    fine = Mesh(mesh.devices.reshape(8, 2, 2, 8, 4), (*DP, *BLK))
    placed = (P(DP, None), P(None, BLK), P(BLK, None), P(BLK, None), P(DP))
    return jax.shard_map(
        body, mesh=fine, in_specs=placed, out_specs=(P(DP, BLK), P(DP, BLK)), check_vma=False
    )
```

```python
import jax
import jax.numpy as jnp
from jax import lax
from jax.sharding import Mesh
from jax.sharding import PartitionSpec as P

DP = ("y", "xl", "core")
BLK = ("z", "xh")
CHIPS = ("core", "z", "xh")

SCALE = 10.0
BIAS = -5.0
EPS = 1e-06
BF16 = jnp.bfloat16
F32 = jnp.float32


def exchange(x, axes, groups=None):
    return lax.all_to_all(x, axes, 0, 0, axis_index_groups=groups, tiled=True)


def to_all(x, n):
    return jnp.broadcast_to(x[None], (n, *x.shape))


def blk_groups(n_z, n_xh):
    zero = [[(z, xh) for z in range(n_z)] for xh in range(n_xh)]
    fine = n_z // n_xh
    one = [[(zh * fine + zl, xh) for zl in range(fine) for xh in range(n_xh)] for zh in range(n_xh)]
    grids = [[[core * n_z * n_xh + z * n_xh + xh for z, xh in row] for row in grid] for core, grid in enumerate((zero, one))]
    first = [list(column) for grid in grids for column in zip(*grid)]
    second = [row for grid in grids for row in grid]
    return first, second


def place(core, n_z, n_xh, z, xh):
    flat = z * n_xh + xh
    return jnp.where(core == 0, xh, flat // n_z), jnp.where(core == 0, z, flat % n_z)


def activate(values):
    return jax.nn.gelu(values, approximate=True)


def body(captions, w_in, w_out, images, pairs):
    rows, width = captions.shape
    n_z, n_xh, n_dp = lax.axis_size("z"), lax.axis_size("xh"), lax.axis_size(DP)
    n_core = lax.axis_size("core")
    core = lax.axis_index("core")
    first, second = blk_groups(n_z, n_xh)
    per_first = rows // n_xh
    own = per_first // n_z
    img_block = images.shape[0]
    img_part = img_block // n_core

    img = lax.dynamic_slice_in_dim(images, core * img_part, img_part, 0).astype(F32)
    img = (img * lax.rsqrt(jnp.sum(img * img, axis=1, keepdims=True) + EPS)).astype(BF16)

    pre_act = jnp.dot(captions, w_in, preferred_element_type=F32)
    hidden = activate(pre_act).astype(BF16)
    partial = jnp.dot(hidden, w_out, preferred_element_type=F32).astype(BF16)

    sent = jnp.concatenate([partial.reshape(n_xh, per_first, width), to_all(img, n_xh)], axis=1)
    got = exchange(sent, CHIPS, first)
    partial = jnp.sum(got[:, :per_first].astype(F32), axis=0).astype(BF16)
    img = got[:, per_first:].reshape(n_xh * img_part, width)
    sent = jnp.concatenate([partial.reshape(n_z, own, width), to_all(img, n_z)], axis=1)
    got = exchange(sent, CHIPS, second)
    img = got[:, own:].reshape(-1, width)
    other_img = lax.ppermute(img, "core", [(i, n_core - 1 - i) for i in range(n_core)])
    embedding = jnp.sum(got[:, :own].astype(F32), axis=0)

    inv_norm = lax.rsqrt(jnp.sum(embedding * embedding, axis=1, keepdims=True) + EPS)
    unit_dir = embedding * inv_norm
    unit_half = unit_dir.astype(BF16)

    at_first, at_second = place(core, n_z, n_xh, lax.axis_index("z"), lax.axis_index("xh"))
    pair = lax.dynamic_slice_in_dim(pairs, at_first * per_first + at_second * own, own, 0)[:, None]
    n = lax.broadcasted_iota(jnp.int32, (1, img.shape[0]), 1)
    slot, row = n // img_part, n % img_part

    def half_grad(img, core):
        block = jnp.where(core == 0, slot, (slot % n_xh) * n_z + slot // n_xh)
        logits = (
            SCALE * lax.dot_general(unit_half, img, (((1,), (1,)), ((), ())), preferred_element_type=F32) + BIAS
        )
        label = (pair == block * img_block + core * img_part + row).astype(F32)
        mismatch = (jax.nn.sigmoid(logits) - label).astype(BF16)
        return jnp.dot(mismatch, img, preferred_element_type=F32)

    unit_grad = SCALE * (half_grad(img, core) + half_grad(other_img, n_core - 1 - core))

    embed_half = (
        (unit_grad - unit_dir * jnp.sum(unit_dir * unit_grad, axis=1, keepdims=True)) * inv_norm
    ).astype(BF16)
    got = exchange(to_all(embed_half, n_z), CHIPS, second).reshape(per_first, width)
    embed_half = exchange(to_all(got, n_xh), CHIPS, first).reshape(rows, width)

    hidden_grad = lax.dot_general(embed_half, w_out, (((1,), (1,)), ((), ())), preferred_element_type=F32)
    _, pullback = jax.vjp(activate, pre_act)
    preact_grad = pullback(hidden_grad)[0].astype(BF16)
    grad_in = lax.dot_general(captions, preact_grad, (((0,), (0,)), ((), ())), preferred_element_type=F32)
    grad_out = lax.dot_general(embed_half, hidden, (((0,), (0,)), ((), ())), preferred_element_type=F32)
    share = width // n_dp
    sent = jnp.concatenate(
        [grad_in.astype(BF16).reshape(n_dp, share, -1), grad_out.astype(BF16).reshape(n_dp, share, -1)], axis=1
    )
    total = jnp.sum(exchange(sent, DP).astype(F32), axis=0)
    return total[:share], total[share:]


def solution(mesh):
    fine = Mesh(mesh.devices.reshape(8, 2, 2, 8, 4), (*DP, *BLK))
    placed = (P(DP, None), P(None, BLK), P(BLK, None), P(BLK, None), P(DP))
    return jax.shard_map(
        body, mesh=fine, in_specs=placed, out_specs=(P(DP, BLK), P(DP, BLK)), check_vma=False
    )
```

```python
import functools

import jax
import jax.numpy as jnp
from jax import lax
from jax.experimental import pallas as pl
from jax.experimental.pallas import tpu as pltpu
from jax.sharding import Mesh
from jax.sharding import PartitionSpec as P

DP = ("y", "xl", "core")
BLK = ("z", "xh")
CHIPS = ("core", "z", "xh")

SCALE = 10.0
BIAS = -5.0
EPS = 1e-06
BF16 = jnp.bfloat16
F32 = jnp.float32


def exchange(x, axes, groups=None):
    return lax.all_to_all(x, axes, 0, 0, axis_index_groups=groups, tiled=True)


def to_all(x, n):
    return jnp.broadcast_to(x[None], (n, *x.shape))


def blk_groups(n_z, n_xh):
    zero = [[(z, xh) for z in range(n_z)] for xh in range(n_xh)]
    fine = n_z // n_xh
    one = [[(zh * fine + zl, xh) for zl in range(fine) for xh in range(n_xh)] for zh in range(n_xh)]
    grids = [[[core * n_z * n_xh + z * n_xh + xh for z, xh in row] for row in grid] for core, grid in enumerate((zero, one))]
    first = [list(column) for grid in grids for column in zip(*grid)]
    second = [row for grid in grids for row in grid]
    return first, second


def place(core, n_z, n_xh, z, xh):
    flat = z * n_xh + xh
    return jnp.where(core == 0, xh, flat // n_z), jnp.where(core == 0, z, flat % n_z)


def activate(values):
    return jax.nn.gelu(values, approximate=True)


def half_grad(core, geometry, unit_half, pair, img):
    n_z, n_xh, img_block, img_part = geometry
    n = lax.broadcasted_iota(jnp.int32, (1, img.shape[0]), 1)
    slot, row = n // img_part, n % img_part
    block = jnp.where(core == 0, slot, (slot % n_xh) * n_z + slot // n_xh)
    logits = SCALE * lax.dot_general(unit_half, img, (((1,), (1,)), ((), ())), preferred_element_type=F32) + BIAS
    label = (pair == block * img_block + core * img_part + row).astype(F32)
    mismatch = (jax.nn.sigmoid(logits) - label).astype(BF16)
    return jnp.dot(mismatch, img, preferred_element_type=F32)


def own_kernel(geometry, core_ref, part_ref, pair_ref, img_ref, dir_ref, norm_ref, grad_ref):
    embedding = part_ref[0].astype(F32)
    for k in range(1, part_ref.shape[0]):
        embedding += part_ref[k].astype(F32)
    inv_norm = lax.rsqrt(jnp.sum(embedding * embedding, axis=1, keepdims=True) + EPS)
    unit_dir = embedding * inv_norm
    dir_ref[...] = unit_dir
    norm_ref[...] = jnp.broadcast_to(inv_norm, norm_ref.shape)
    grad_ref[...] = half_grad(core_ref[0], geometry, unit_dir.astype(BF16), pair_ref[:, :1], img_ref[...])


def other_kernel(geometry, core_ref, dir_ref, norm_ref, grad_ref, pair_ref, img_ref, out_ref):
    unit_dir = dir_ref[...]
    more = half_grad(1 - core_ref[0], geometry, unit_dir.astype(BF16), pair_ref[:, :1], img_ref[...])
    unit_grad = SCALE * (grad_ref[...] + more)
    along = jnp.sum(unit_dir * unit_grad, axis=1, keepdims=True)
    embed_half = ((unit_grad - unit_dir * along) * norm_ref[:, :1]).astype(BF16)
    for k in range(out_ref.shape[0]):
        out_ref[k] = embed_half


def call(kernel, outs, flops, *args):
    whole = pl.BlockSpec(memory_space=pltpu.VMEM)
    return pl.pallas_call(
        kernel,
        out_shape=outs,
        in_specs=[pl.BlockSpec(memory_space=pltpu.SMEM)] + [whole] * (len(args) - 1),
        out_specs=jax.tree.map(lambda _: whole, outs),
        compiler_params=pltpu.CompilerParams(vmem_limit_bytes=16 * 1024 * 1024),
        cost_estimate=pl.CostEstimate(flops=flops, bytes_accessed=3_000_000, transcendentals=0),
    )(*args)


def body(captions, w_in, w_out, images, pairs):
    rows, width = captions.shape
    n_z, n_xh, n_dp = lax.axis_size("z"), lax.axis_size("xh"), lax.axis_size(DP)
    n_core = lax.axis_size("core")
    core = lax.axis_index("core")
    first, second = blk_groups(n_z, n_xh)
    per_first = rows // n_xh
    own = per_first // n_z
    img_block = images.shape[0]
    img_part = img_block // n_core

    img = lax.dynamic_slice_in_dim(images, core * img_part, img_part, 0)

    pre_act = jnp.dot(captions, w_in, preferred_element_type=F32)
    hidden = activate(pre_act).astype(BF16)
    partial = jnp.dot(hidden, w_out, preferred_element_type=F32).astype(BF16)

    sent = jnp.concatenate([partial.reshape(n_xh, per_first, width), to_all(img, n_xh)], axis=1)
    got = exchange(sent, CHIPS, first)
    partial = jnp.sum(got[:, :per_first].astype(F32), axis=0).astype(BF16)
    img = got[:, per_first:].reshape(n_xh * img_part, width).astype(F32)
    img = (img * lax.rsqrt(jnp.sum(img * img, axis=1, keepdims=True) + EPS)).astype(BF16)
    sent = jnp.concatenate([partial.reshape(n_z, own, width), to_all(img, n_z)], axis=1)
    got = exchange(sent, CHIPS, second)
    partial, img = lax.optimization_barrier((got[:, :own], got[:, own:]))
    img = img.reshape(-1, width)
    other_img = lax.ppermute(img, "core", [(i, n_core - 1 - i) for i in range(n_core)])

    at_first, at_second = place(core, n_z, n_xh, lax.axis_index("z"), lax.axis_index("xh"))
    pair = lax.dynamic_slice_in_dim(pairs, at_first * per_first + at_second * own, own, 0)
    pair = jnp.broadcast_to(pair[:, None], (own, 128))
    geometry = (n_z, n_xh, img_block, img_part)
    here = core.reshape(1).astype(jnp.int32)
    flops = 4 * own * img.shape[0] * width
    row = jax.ShapeDtypeStruct((own, width), F32)
    unit_dir, inv_norm, grad = call(
        functools.partial(own_kernel, geometry),
        (row, jax.ShapeDtypeStruct((own, 128), F32), row),
        flops,
        here,
        partial,
        pair,
        img,
    )
    sent = call(
        functools.partial(other_kernel, geometry),
        jax.ShapeDtypeStruct((n_z, own, width), BF16),
        flops,
        here,
        unit_dir,
        inv_norm,
        grad,
        pair,
        other_img,
    )
    got = exchange(sent, CHIPS, second).reshape(per_first, width)
    embed_half = exchange(to_all(got, n_xh), CHIPS, first).reshape(rows, width)

    hidden_grad = lax.dot_general(embed_half, w_out, (((1,), (1,)), ((), ())), preferred_element_type=F32)
    _, pullback = jax.vjp(activate, pre_act)
    preact_grad = pullback(hidden_grad)[0].astype(BF16)
    grad_in = lax.dot_general(captions, preact_grad, (((0,), (0,)), ((), ())), preferred_element_type=F32)
    grad_out = lax.dot_general(embed_half, hidden, (((0,), (0,)), ((), ())), preferred_element_type=F32)
    share = width // n_dp
    sent = jnp.concatenate(
        [grad_in.astype(BF16).reshape(n_dp, share, -1), grad_out.astype(BF16).reshape(n_dp, share, -1)], axis=1
    )
    total = jnp.sum(exchange(sent, DP).astype(F32), axis=0)
    return total[:share], total[share:]


def solution(mesh):
    fine = Mesh(mesh.devices.reshape(8, 2, 2, 8, 4), (*DP, *BLK))
    placed = (P(DP, None), P(None, BLK), P(BLK, None), P(BLK, None), P(DP))
    return jax.shard_map(
        body, mesh=fine, in_specs=placed, out_specs=(P(DP, BLK), P(DP, BLK)), check_vma=False
    )
```

```python
import functools
import math

import jax
import jax.numpy as jnp
from jax import lax
from jax.experimental import pallas as pl
from jax.experimental.pallas import tpu as pltpu
from jax.sharding import Mesh
from jax.sharding import PartitionSpec as P

DP = ("y", "xl", "core")
BLK = ("z", "xh")
CHIPS = ("core", "z", "xh")

SCALE = 10.0
BIAS = -5.0
EPS = 1e-06
CURVE = math.sqrt(2.0 / math.pi)
CUBIC = 0.044715
GRANT = 60 * 1024 * 1024
BF16 = jnp.bfloat16
F32 = jnp.float32


def exchange(x, axes, groups=None):
    return lax.all_to_all(x, axes, 0, 0, axis_index_groups=groups, tiled=True)


def to_all(x, n):
    return jnp.broadcast_to(x[None], (n, *x.shape))


def blk_groups(n_z, n_xh):
    zero = [[(z, xh) for z in range(n_z)] for xh in range(n_xh)]
    fine = n_z // n_xh
    one = [[(zh * fine + zl, xh) for zl in range(fine) for xh in range(n_xh)] for zh in range(n_xh)]
    grids = [[[core * n_z * n_xh + z * n_xh + xh for z, xh in row] for row in grid] for core, grid in enumerate((zero, one))]
    first = [list(column) for grid in grids for column in zip(*grid)]
    second = [row for grid in grids for row in grid]
    return first, second


def bend(v):
    return jnp.tanh(CURVE * (v + CUBIC * (v * v * v)))


def place(core, n_z, n_xh, z, xh):
    flat = z * n_xh + xh
    return jnp.where(core == 0, xh, flat // n_z), jnp.where(core == 0, z, flat % n_z)


def forward_kernel(
    per_first, img_part, core_ref, captions_hbm, w_in_hbm, w_out_hbm, images_hbm, out_hbm, pre_hbm,
    captions_ref, w_in_ref, w_out_ref, img_ref, out_ref, pre_ref, sems
):
    n = out_ref.shape[0]
    start = pl.multiple_of(core_ref[0] * img_part, img_part)
    blocks = [pl.ds(k * per_first, per_first) for k in range(n)]
    fetch_in = pltpu.make_async_copy(w_in_hbm, w_in_ref, sems.at[0])
    fetch_out = pltpu.make_async_copy(w_out_hbm, w_out_ref, sems.at[1])
    fetch_img = pltpu.make_async_copy(images_hbm.at[pl.ds(start, img_part)], img_ref, sems.at[2])
    fetches = [
        pltpu.make_async_copy(captions_hbm.at[at], captions_ref.at[at], sems.at[3 + k]) for k, at in enumerate(blocks)
    ]
    for copy in (fetch_in, fetches[0], fetch_out, fetch_img, *fetches[1:]):
        copy.start()
    stores = []
    fetch_in.wait()
    for k, at in enumerate(blocks):
        fetches[k].wait()
        pre_act = jnp.dot(captions_ref[at, :], w_in_ref[...], preferred_element_type=F32)
        pre_ref[at, :] = pre_act
        hidden = (0.5 * pre_act * (1.0 + bend(pre_act))).astype(BF16)
        if k == 0:
            fetch_out.wait()
            fetch_img.wait()
        out_ref[k, :per_first] = jnp.dot(hidden, w_out_ref[...], preferred_element_type=F32).astype(BF16)
        out_ref[k, per_first:] = img_ref[...]
        stores.append(pltpu.make_async_copy(out_ref.at[k], out_hbm.at[k], sems.at[3 + n + k]))
        stores.append(pltpu.make_async_copy(pre_ref.at[at], pre_hbm.at[at], sems.at[3 + 2 * n + k]))
        stores[-2].start()
        stores[-1].start()
    for copy in stores:
        copy.wait()


def backward_kernel(share, core_ref, captions_ref, embed_ref, w_out_ref, pre_ref, mine_ref, other_ref):
    embed_half = embed_ref[...]
    hidden_grad = lax.dot_general(embed_half, w_out_ref[...], (((1,), (1,)), ((), ())), preferred_element_type=F32)
    v = pre_ref[...]
    t = bend(v)
    hidden = (0.5 * v * (1.0 + t)).astype(BF16)
    slope = 0.5 * (1.0 + t) + 0.5 * v * (1.0 - t * t) * (CURVE * (1.0 + 3.0 * CUBIC * v * v))
    preact_grad = (hidden_grad * slope).astype(BF16)
    over_rows = (((0,), (0,)), ((), ()))
    grad_in = lax.dot_general(preact_grad, captions_ref[...], over_rows, preferred_element_type=F32).T
    grad_out = lax.dot_general(hidden, embed_half, over_rows, preferred_element_type=F32).T
    zero = core_ref[0] == 0
    for at, grad in ((0, grad_in), (share, grad_out)):
        for q in range(mine_ref.shape[0]):
            even = grad[2 * q * share : (2 * q + 1) * share]
            odd = grad[(2 * q + 1) * share : (2 * q + 2) * share]
            mine_ref[q, at : at + share] = jnp.where(zero, even, odd)
            other_ref[q, at : at + share] = jnp.where(zero, odd, even)


def half_grad(core, geometry, unit_half, pair, img):
    n_z, n_xh, img_block, img_part = geometry
    n = lax.broadcasted_iota(jnp.int32, (1, img.shape[0]), 1)
    slot, row = n // img_part, n % img_part
    block = jnp.where(core == 0, slot, (slot % n_xh) * n_z + slot // n_xh)
    logits = SCALE * lax.dot_general(unit_half, img, (((1,), (1,)), ((), ())), preferred_element_type=F32) + BIAS
    label = (pair == block * img_block + core * img_part + row).astype(F32)
    mismatch = (jax.nn.sigmoid(logits) - label).astype(BF16)
    return jnp.dot(mismatch, img, preferred_element_type=F32)


def own_kernel(geometry, core_ref, sum_ref, pair_ref, img_ref, dir_ref, norm_ref, grad_ref):
    embedding = sum_ref[...]
    inv_norm = lax.rsqrt(jnp.sum(embedding * embedding, axis=1, keepdims=True) + EPS)
    unit_dir = embedding * inv_norm
    dir_ref[...] = unit_dir
    norm_ref[...] = jnp.broadcast_to(inv_norm, norm_ref.shape)
    grad_ref[...] = half_grad(core_ref[0], geometry, unit_dir.astype(BF16), pair_ref[:, :1], img_ref[...])


def other_kernel(geometry, core_ref, dir_ref, norm_ref, grad_ref, pair_ref, img_ref, out_ref):
    unit_dir = dir_ref[...]
    more = half_grad(1 - core_ref[0], geometry, unit_dir.astype(BF16), pair_ref[:, :1], img_ref[...])
    unit_grad = SCALE * (grad_ref[...] + more)
    along = jnp.sum(unit_dir * unit_grad, axis=1, keepdims=True)
    embed_half = ((unit_grad - unit_dir * along) * norm_ref[:, :1]).astype(BF16)
    for k in range(out_ref.shape[0]):
        out_ref[k] = embed_half


def call(kernel, outs, flops, *args, place=pltpu.VMEM, scratch=(), grant=16 * 1024 * 1024):
    whole = pl.BlockSpec(memory_space=place)
    return pl.pallas_call(
        kernel,
        out_shape=outs,
        in_specs=[pl.BlockSpec(memory_space=pltpu.SMEM)] + [whole] * (len(args) - 1),
        out_specs=jax.tree.map(lambda _: whole, outs),
        scratch_shapes=scratch,
        compiler_params=pltpu.CompilerParams(vmem_limit_bytes=grant),
        cost_estimate=pl.CostEstimate(flops=flops, bytes_accessed=3_000_000, transcendentals=0),
    )(*args)


def body(captions, w_in, w_out, images, pairs):
    rows, width = captions.shape
    n_z, n_xh, n_dp = lax.axis_size("z"), lax.axis_size("xh"), lax.axis_size(DP)
    n_core = lax.axis_size("core")
    core = lax.axis_index("core")
    swap = [(i, n_core - 1 - i) for i in range(n_core)]
    first, second = blk_groups(n_z, n_xh)
    per_first = rows // n_xh
    own = per_first // n_z
    img_block = images.shape[0]
    img_part = img_block // n_core

    here = core.reshape(1).astype(jnp.int32)
    sums = jax.ShapeDtypeStruct((n_xh, per_first + img_part, width), BF16)
    acts = jax.ShapeDtypeStruct((rows, w_in.shape[1]), F32)
    sent, pre_act = call(
        functools.partial(forward_kernel, per_first, img_part),
        (sums, acts),
        4 * rows * width * w_in.shape[1],
        here,
        captions,
        w_in,
        w_out,
        images,
        place=pltpu.HBM,
        grant=GRANT,
        scratch=[
            pltpu.VMEM(captions.shape, BF16),
            pltpu.VMEM(w_in.shape, BF16),
            pltpu.VMEM(w_out.shape, BF16),
            pltpu.VMEM((img_part, width), BF16),
            pltpu.VMEM(sums.shape, BF16),
            pltpu.VMEM(acts.shape, F32),
            pltpu.SemaphoreType.DMA((3 + 3 * n_xh,)),
        ],
    )
    got = exchange(sent, CHIPS, first)
    partial = jnp.sum(got[:, :per_first].astype(F32), axis=0).astype(BF16)
    img = got[:, per_first:].reshape(n_xh * img_part, width).astype(F32)
    img = (img * lax.rsqrt(jnp.sum(img * img, axis=1, keepdims=True) + EPS)).astype(BF16)
    sent = jnp.concatenate([partial.reshape(n_z, own, width), to_all(img, n_z)], axis=1)
    got = exchange(sent, CHIPS, second)
    embedding = jnp.sum(got[:, :own].astype(F32), axis=0)
    embedding, img = lax.optimization_barrier((embedding, got[:, own:].reshape(-1, width)))
    other_img = lax.ppermute(img, "core", swap)

    at_first, at_second = place(core, n_z, n_xh, lax.axis_index("z"), lax.axis_index("xh"))
    pair = lax.dynamic_slice_in_dim(pairs, at_first * per_first + at_second * own, own, 0)
    pair = jnp.broadcast_to(pair[:, None], (own, 128))
    geometry = (n_z, n_xh, img_block, img_part)
    flops = 4 * own * img.shape[0] * width
    row = jax.ShapeDtypeStruct((own, width), F32)
    unit_dir, inv_norm, grad = call(
        functools.partial(own_kernel, geometry),
        (row, jax.ShapeDtypeStruct((own, 128), F32), row),
        flops,
        here,
        embedding,
        pair,
        img,
    )
    sent = call(
        functools.partial(other_kernel, geometry),
        jax.ShapeDtypeStruct((n_z, own, width), BF16),
        flops,
        here,
        unit_dir,
        inv_norm,
        grad,
        pair,
        other_img,
    )
    got = exchange(sent, CHIPS, second).reshape(per_first, width)
    embed_half = exchange(to_all(got, n_xh), CHIPS, first).reshape(rows, width)

    share = width // n_dp
    grads = jax.ShapeDtypeStruct((n_dp // n_core, 2 * share, w_in.shape[1]), F32)
    mine, other = call(
        functools.partial(backward_kernel, share),
        (grads, grads),
        6 * rows * width * w_in.shape[1],
        here,
        captions,
        embed_half,
        w_out,
        pre_act,
    )
    mine = mine + lax.ppermute(other, "core", swap)
    total = jnp.sum(exchange(mine.astype(BF16), ("y", "xl")).astype(F32), axis=0)
    return total[:share], total[share:]


def solution(mesh):
    fine = Mesh(mesh.devices.reshape(8, 2, 2, 8, 4), (*DP, *BLK))
    placed = (P(DP, None), P(None, BLK), P(BLK, None), P(BLK, None), P(DP))
    return jax.shard_map(
        body, mesh=fine, in_specs=placed, out_specs=(P(DP, BLK), P(DP, BLK)), check_vma=False
    )
```

```python
import functools
import math

import jax
import jax.numpy as jnp
from jax import lax
from jax.experimental import pallas as pl
from jax.experimental.pallas import tpu as pltpu
from jax.sharding import Mesh
from jax.sharding import PartitionSpec as P

DP = ("y", "xl", "core")
BLK = ("z", "xh")
CHIPS = ("core", "z", "xh")

SCALE = 10.0
BIAS = -5.0
EPS = 1e-06
CURVE = math.sqrt(2.0 / math.pi)
CUBIC = 0.044715
GRANT = 60 * 1024 * 1024
BF16 = jnp.bfloat16
F32 = jnp.float32


def exchange(x, axes, groups=None):
    return lax.all_to_all(x, axes, 0, 0, axis_index_groups=groups, tiled=True)


def to_all(x, n):
    return jnp.broadcast_to(x[None], (n, *x.shape))


def blk_groups(n_z, n_xh):
    zero = [[(z, xh) for z in range(n_z)] for xh in range(n_xh)]
    fine = n_z // n_xh
    one = [[(zh * fine + zl, xh) for zl in range(fine) for xh in range(n_xh)] for zh in range(n_xh)]
    grids = [[[core * n_z * n_xh + z * n_xh + xh for z, xh in row] for row in grid] for core, grid in enumerate((zero, one))]
    first = [list(column) for grid in grids for column in zip(*grid)]
    second = [row for grid in grids for row in grid]
    return first, second


def bend(v):
    return jnp.tanh(CURVE * (v + CUBIC * (v * v * v)))


def place(core, n_z, n_xh, z, xh):
    flat = z * n_xh + xh
    return jnp.where(core == 0, xh, flat // n_z), jnp.where(core == 0, z, flat % n_z)


def forward_kernel(
    per_first, img_part, core_ref, captions_hbm, w_in_hbm, w_out_hbm, images_hbm, out_hbm, pre_hbm,
    captions_ref, w_in_ref, w_out_ref, img_ref, out_ref, pre_ref, sems
):
    n = out_ref.shape[0] // 2
    half = n * per_first
    start = pl.multiple_of(core_ref[0] * img_part, img_part)
    fetch_in = pltpu.make_async_copy(w_in_hbm, w_in_ref, sems.at[0])
    fetch_out = pltpu.make_async_copy(w_out_hbm, w_out_ref, sems.at[1])
    fetch_img = pltpu.make_async_copy(images_hbm.at[pl.ds(start, img_part)], img_ref, sems.at[2])
    blocks = [pl.ds(k * half, half) for k in range(2)]
    fetches = [
        pltpu.make_async_copy(captions_hbm.at[at], captions_ref.at[at], sems.at[3 + k]) for k, at in enumerate(blocks)
    ]
    for copy in (fetch_in, fetches[0], fetch_out, fetch_img, fetches[1]):
        copy.start()
    stores = []
    fetch_in.wait()
    for k, at in enumerate(blocks):
        fetches[k].wait()
        pre_act = jnp.dot(captions_ref[at, :], w_in_ref[...], preferred_element_type=F32)
        pre_ref[at, :] = pre_act
        hidden = (0.5 * pre_act * (1.0 + bend(pre_act))).astype(BF16)
        if k == 0:
            fetch_out.wait()
            fetch_img.wait()
        total = jnp.dot(hidden, w_out_ref[...], preferred_element_type=F32).astype(BF16)
        for q in range(n):
            out_ref[k * n + q, :per_first] = total[q * per_first : (q + 1) * per_first]
            out_ref[k * n + q, per_first:] = img_ref[...]
        to = pl.ds(k * n, n)
        stores.append(pltpu.make_async_copy(out_ref.at[to], out_hbm.at[to], sems.at[5 + k]))
        stores.append(pltpu.make_async_copy(pre_ref.at[at], pre_hbm.at[at], sems.at[7 + k]))
        stores[-2].start()
        stores[-1].start()
    for copy in stores:
        copy.wait()


def backward_kernel(share, core_ref, captions_ref, embed_ref, w_out_ref, pre_ref, mine_ref, other_ref):
    embed_half = embed_ref[...]
    hidden_grad = lax.dot_general(embed_half, w_out_ref[...], (((1,), (1,)), ((), ())), preferred_element_type=F32)
    v = pre_ref[...]
    t = bend(v)
    hidden = (0.5 * v * (1.0 + t)).astype(BF16)
    slope = 0.5 * (1.0 + t) + 0.5 * v * (1.0 - t * t) * (CURVE * (1.0 + 3.0 * CUBIC * v * v))
    preact_grad = (hidden_grad * slope).astype(BF16)
    over_rows = (((0,), (0,)), ((), ()))
    grad_in = lax.dot_general(preact_grad, captions_ref[...], over_rows, preferred_element_type=F32).T
    grad_out = lax.dot_general(hidden, embed_half, over_rows, preferred_element_type=F32).T
    zero = core_ref[0] == 0
    for at, grad in ((0, grad_in), (share, grad_out)):
        for q in range(mine_ref.shape[0]):
            even = grad[2 * q * share : (2 * q + 1) * share]
            odd = grad[(2 * q + 1) * share : (2 * q + 2) * share]
            mine_ref[q, at : at + share] = jnp.where(zero, even, odd)
            other_ref[q, at : at + share] = jnp.where(zero, odd, even).astype(BF16)


def half_grad(core, geometry, unit_half, pair, img):
    n_z, n_xh, img_block, img_part = geometry
    n = lax.broadcasted_iota(jnp.int32, (1, img.shape[0]), 1)
    slot, row = n // img_part, n % img_part
    block = jnp.where(core == 0, slot, (slot % n_xh) * n_z + slot // n_xh)
    logits = SCALE * lax.dot_general(unit_half, img, (((1,), (1,)), ((), ())), preferred_element_type=F32) + BIAS
    label = (pair == block * img_block + core * img_part + row).astype(F32)
    mismatch = (jax.nn.sigmoid(logits) - label).astype(BF16)
    return jnp.dot(mismatch, img, preferred_element_type=F32)


def own_kernel(geometry, core_ref, sum_ref, pair_ref, img_ref, dir_ref, norm_ref, grad_ref):
    embedding = sum_ref[...]
    inv_norm = lax.rsqrt(jnp.sum(embedding * embedding, axis=1, keepdims=True) + EPS)
    unit_dir = embedding * inv_norm
    dir_ref[...] = unit_dir
    norm_ref[...] = jnp.broadcast_to(inv_norm, norm_ref.shape)
    grad_ref[...] = half_grad(core_ref[0], geometry, unit_dir.astype(BF16), pair_ref[:, :1], img_ref[...])


def other_kernel(geometry, core_ref, dir_ref, norm_ref, grad_ref, pair_ref, img_ref, out_ref):
    unit_dir = dir_ref[...]
    more = half_grad(1 - core_ref[0], geometry, unit_dir.astype(BF16), pair_ref[:, :1], img_ref[...])
    unit_grad = SCALE * (grad_ref[...] + more)
    along = jnp.sum(unit_dir * unit_grad, axis=1, keepdims=True)
    embed_half = ((unit_grad - unit_dir * along) * norm_ref[:, :1]).astype(BF16)
    for k in range(out_ref.shape[0]):
        out_ref[k] = embed_half


def call(kernel, outs, flops, *args, place=pltpu.VMEM, scratch=(), grant=16 * 1024 * 1024):
    whole = pl.BlockSpec(memory_space=place)
    return pl.pallas_call(
        kernel,
        out_shape=outs,
        in_specs=[pl.BlockSpec(memory_space=pltpu.SMEM)] + [whole] * (len(args) - 1),
        out_specs=jax.tree.map(lambda _: whole, outs),
        scratch_shapes=scratch,
        compiler_params=pltpu.CompilerParams(vmem_limit_bytes=grant),
        cost_estimate=pl.CostEstimate(flops=flops, bytes_accessed=3_000_000, transcendentals=0),
    )(*args)


def body(captions, w_in, w_out, images, pairs):
    rows, width = captions.shape
    n_z, n_xh, n_dp = lax.axis_size("z"), lax.axis_size("xh"), lax.axis_size(DP)
    n_core = lax.axis_size("core")
    core = lax.axis_index("core")
    swap = [(i, n_core - 1 - i) for i in range(n_core)]
    first, second = blk_groups(n_z, n_xh)
    per_first = rows // n_xh
    own = per_first // n_z
    img_block = images.shape[0]
    img_part = img_block // n_core

    here = core.reshape(1).astype(jnp.int32)
    sums = jax.ShapeDtypeStruct((n_xh, per_first + img_part, width), BF16)
    acts = jax.ShapeDtypeStruct((rows, w_in.shape[1]), F32)
    sent, pre_act = call(
        functools.partial(forward_kernel, per_first, img_part),
        (sums, acts),
        4 * rows * width * w_in.shape[1],
        here,
        captions,
        w_in,
        w_out,
        images,
        place=pltpu.HBM,
        grant=GRANT,
        scratch=[
            pltpu.VMEM(captions.shape, BF16),
            pltpu.VMEM(w_in.shape, BF16),
            pltpu.VMEM(w_out.shape, BF16),
            pltpu.VMEM((img_part, width), BF16),
            pltpu.VMEM(sums.shape, BF16),
            pltpu.VMEM(acts.shape, F32),
            pltpu.SemaphoreType.DMA((9,)),
        ],
    )
    got = exchange(sent, CHIPS, first)
    partial = jnp.sum(got[:, :per_first].astype(F32), axis=0).astype(BF16)
    img = got[:, per_first:].reshape(n_xh * img_part, width).astype(F32)
    img = (img * lax.rsqrt(jnp.sum(img * img, axis=1, keepdims=True) + EPS)).astype(BF16)
    sent = jnp.concatenate([partial.reshape(n_z, own, width), to_all(img, n_z)], axis=1)
    got = exchange(sent, CHIPS, second)
    embedding = jnp.sum(got[:, :own].astype(F32), axis=0)
    embedding, img = lax.optimization_barrier((embedding, got[:, own:].reshape(-1, width)))
    other_img = lax.ppermute(img, "core", swap)

    at_first, at_second = place(core, n_z, n_xh, lax.axis_index("z"), lax.axis_index("xh"))
    pair = lax.dynamic_slice_in_dim(pairs, at_first * per_first + at_second * own, own, 0)
    pair = jnp.broadcast_to(pair[:, None], (own, 128))
    geometry = (n_z, n_xh, img_block, img_part)
    flops = 4 * own * img.shape[0] * width
    row = jax.ShapeDtypeStruct((own, width), F32)
    unit_dir, inv_norm, grad = call(
        functools.partial(own_kernel, geometry),
        (row, jax.ShapeDtypeStruct((own, 128), F32), row),
        flops,
        here,
        embedding,
        pair,
        img,
    )
    sent = call(
        functools.partial(other_kernel, geometry),
        jax.ShapeDtypeStruct((n_z, own, width), BF16),
        flops,
        here,
        unit_dir,
        inv_norm,
        grad,
        pair,
        other_img,
    )
    got = exchange(sent, CHIPS, second).reshape(per_first, width)
    embed_half = exchange(to_all(got, n_xh), CHIPS, first).reshape(rows, width)

    share = width // n_dp
    grads = (n_dp // n_core, 2 * share, w_in.shape[1])
    mine, other = call(
        functools.partial(backward_kernel, share),
        (jax.ShapeDtypeStruct(grads, F32), jax.ShapeDtypeStruct(grads, BF16)),
        6 * rows * width * w_in.shape[1],
        here,
        captions,
        embed_half,
        w_out,
        pre_act,
    )
    mine = mine + lax.ppermute(other, "core", swap).astype(F32)
    total = jnp.sum(exchange(mine.astype(BF16), ("y", "xl")).astype(F32), axis=0)
    return total[:share], total[share:]


def solution(mesh):
    fine = Mesh(mesh.devices.reshape(8, 2, 2, 8, 4), (*DP, *BLK))
    placed = (P(DP, None), P(None, BLK), P(BLK, None), P(BLK, None), P(DP))
    return jax.shard_map(
        body, mesh=fine, in_specs=placed, out_specs=(P(DP, BLK), P(DP, BLK)), check_vma=False
    )
```

```python
import functools
import math

import jax
import jax.numpy as jnp
from jax import lax
from jax.experimental import pallas as pl
from jax.experimental.pallas import tpu as pltpu
from jax.sharding import Mesh
from jax.sharding import PartitionSpec as P

DP = ("y", "xl", "core")
BLK = ("z", "xh")
CHIPS = ("core", "z", "xh")

SCALE = 10.0
BIAS = -5.0
EPS = 1e-06
DIGIT = 32
CURVE = math.sqrt(2.0 / math.pi)
CUBIC = 0.044715
GRANT = 60 * 1024 * 1024
BF16 = jnp.bfloat16
F32 = jnp.float32


def exchange(x, axes, groups=None):
    return lax.all_to_all(x, axes, 0, 0, axis_index_groups=groups, tiled=True)


def to_all(x, n):
    return jnp.broadcast_to(x[None], (n, *x.shape))


def blk_groups(n_z, n_xh):
    zero = [[(z, xh) for z in range(n_z)] for xh in range(n_xh)]
    fine = n_z // n_xh
    one = [[(zh * fine + zl, xh) for zl in range(fine) for xh in range(n_xh)] for zh in range(n_xh)]
    grids = [[[core * n_z * n_xh + z * n_xh + xh for z, xh in row] for row in grid] for core, grid in enumerate((zero, one))]
    first = [list(column) for grid in grids for column in zip(*grid)]
    second = [row for grid in grids for row in grid]
    return first, second


def bend(v):
    return jnp.tanh(CURVE * (v + CUBIC * (v * v * v)))


def place(core, n_z, n_xh, z, xh):
    flat = z * n_xh + xh
    return jnp.where(core == 0, xh, flat // n_z), jnp.where(core == 0, z, flat % n_z)


def forward_kernel(
    per_first, img_part, where, captions_hbm, w_in_hbm, w_out_hbm, images_hbm, out_hbm, pre_hbm,
    captions_ref, w_in_ref, w_out_ref, img_ref, out_ref, pre_ref, sems
):
    n = out_ref.shape[0] // 2
    half = n * per_first
    start = pl.multiple_of(where[0] * img_part, img_part)
    fetch_in = pltpu.make_async_copy(w_in_hbm, w_in_ref, sems.at[0])
    fetch_out = pltpu.make_async_copy(w_out_hbm, w_out_ref, sems.at[1])
    fetch_img = pltpu.make_async_copy(images_hbm.at[pl.ds(start, img_part)], img_ref, sems.at[2])
    blocks = [pl.ds(k * half, half) for k in range(2)]
    fetches = [
        pltpu.make_async_copy(captions_hbm.at[at], captions_ref.at[at], sems.at[3 + k]) for k, at in enumerate(blocks)
    ]
    for copy in (fetch_in, fetches[0], fetch_out, fetch_img, fetches[1]):
        copy.start()
    stores = []
    fetch_in.wait()
    for k, at in enumerate(blocks):
        fetches[k].wait()
        pre_act = jnp.dot(captions_ref[at, :], w_in_ref[...], preferred_element_type=F32)
        pre_ref[at, :] = pre_act
        hidden = (0.5 * pre_act * (1.0 + bend(pre_act))).astype(BF16)
        if k == 0:
            fetch_out.wait()
            fetch_img.wait()
        total = jnp.dot(hidden, w_out_ref[...], preferred_element_type=F32).astype(BF16)
        for q in range(n):
            out_ref[k * n + q, :per_first] = total[q * per_first : (q + 1) * per_first]
            out_ref[k * n + q, per_first:] = img_ref[...]
        to = pl.ds(k * n, n)
        stores.append(pltpu.make_async_copy(out_ref.at[to], out_hbm.at[to], sems.at[5 + k]))
        stores.append(pltpu.make_async_copy(pre_ref.at[at], pre_hbm.at[at], sems.at[7 + k]))
        stores[-2].start()
        stores[-1].start()
    for copy in stores:
        copy.wait()


def backward_kernel(share, where, captions_ref, embed_ref, w_out_ref, pre_ref, mine_ref, other_ref):
    embed_half = embed_ref[...]
    hidden_grad = lax.dot_general(embed_half, w_out_ref[...], (((1,), (1,)), ((), ())), preferred_element_type=F32)
    v = pre_ref[...]
    t = bend(v)
    hidden = (0.5 * v * (1.0 + t)).astype(BF16)
    slope = 0.5 * (1.0 + t) + 0.5 * v * (1.0 - t * t) * (CURVE * (1.0 + 3.0 * CUBIC * v * v))
    preact_grad = (hidden_grad * slope).astype(BF16)
    over_rows = (((0,), (0,)), ((), ()))
    grad_in = lax.dot_general(preact_grad, captions_ref[...], over_rows, preferred_element_type=F32).T
    grad_out = lax.dot_general(hidden, embed_half, over_rows, preferred_element_type=F32).T
    zero = where[0] % 2 == 0
    for at, grad in ((0, grad_in), (share, grad_out)):
        for q in range(mine_ref.shape[0]):
            even = grad[2 * q * share : (2 * q + 1) * share]
            odd = grad[(2 * q + 1) * share : (2 * q + 2) * share]
            mine_ref[q, at : at + share] = jnp.where(zero, even, odd)
            other_ref[q, at : at + share] = jnp.where(zero, odd, even).astype(BF16)


def half_grad(spot, geometry, unit_half, pair, img):
    n_z, n_xh, img_block, img_part = geometry
    n = lax.broadcasted_iota(jnp.int32, (1, img.shape[0]), 1)
    slot, row = n // img_part, n % img_part
    block = jnp.where(spot % 2 == 0, slot, (slot % n_xh) * n_z + slot // n_xh)
    logits = SCALE * lax.dot_general(unit_half, img, (((1,), (1,)), ((), ())), preferred_element_type=F32) + BIAS
    column = block * img_block + spot * img_part + row
    mismatch = (jax.nn.sigmoid(logits) - (pair == column).astype(F32)).astype(BF16)
    return jnp.dot(mismatch, img, preferred_element_type=F32)


def norm_kernel(where, sum_ref, pair_ref, dir_ref, norm_ref, unit_ref):
    embedding = sum_ref[...]
    width = embedding.shape[1]
    inv_norm = lax.rsqrt(jnp.sum(embedding * embedding, axis=1, keepdims=True) + EPS)
    unit_dir = embedding * inv_norm
    dir_ref[...] = unit_dir
    norm_ref[...] = jnp.broadcast_to(inv_norm, norm_ref.shape)
    pair = pair_ref[...]
    lane = lax.broadcasted_iota(jnp.int32, pair.shape, 1)
    digits = jnp.where(lane == 0, pair // DIGIT, jnp.where(lane == 1, pair % DIGIT, 0))
    unit_ref[:, :width] = unit_dir.astype(BF16)
    unit_ref[:, width:] = digits.astype(F32).astype(BF16)


def score_kernel(geometry, where, unit_ref, mine_ref, other_ref, grad_ref):
    width = grad_ref.shape[1]
    spot = where[0]
    digits = unit_ref[:, width:].astype(F32)
    pair = (digits[:, :1] * DIGIT + digits[:, 1:2]).astype(jnp.int32)
    unit_half = unit_ref[:, :width]
    grad_ref[...] = half_grad(spot, geometry, unit_half, pair, mine_ref[...]) + half_grad(
        spot + 1 - 2 * (spot % 2), geometry, unit_half, pair, other_ref[...]
    )


def project_kernel(where, dir_ref, norm_ref, mine_ref, other_ref, out_ref):
    unit_dir = dir_ref[...]
    unit_grad = SCALE * (mine_ref[...] + other_ref[...])
    along = jnp.sum(unit_dir * unit_grad, axis=1, keepdims=True)
    embed_half = ((unit_grad - unit_dir * along) * norm_ref[:, :1]).astype(BF16)
    for k in range(out_ref.shape[0]):
        out_ref[k] = embed_half


def call(kernel, outs, flops, *args, place=pltpu.VMEM, scratch=(), grant=16 * 1024 * 1024):
    whole = pl.BlockSpec(memory_space=place)
    return pl.pallas_call(
        kernel,
        out_shape=outs,
        in_specs=[pl.BlockSpec(memory_space=pltpu.SMEM)] + [whole] * (len(args) - 1),
        out_specs=jax.tree.map(lambda _: whole, outs),
        scratch_shapes=scratch,
        compiler_params=pltpu.CompilerParams(vmem_limit_bytes=grant),
        cost_estimate=pl.CostEstimate(flops=flops, bytes_accessed=3_000_000, transcendentals=0),
    )(*args)


def body(captions, w_in, w_out, images, pairs):
    rows, width = captions.shape
    n_z, n_xh, n_dp = lax.axis_size("z"), lax.axis_size("xh"), lax.axis_size(DP)
    n_core = lax.axis_size("core")
    core = lax.axis_index("core")
    swap = [(i, n_core - 1 - i) for i in range(n_core)]
    first, second = blk_groups(n_z, n_xh)
    per_first = rows // n_xh
    own = per_first // n_z
    img_block = images.shape[0]
    img_part = img_block // (n_core * lax.axis_size("xl"))

    here = lax.axis_index(("xl", "core")).reshape(1).astype(jnp.int32)
    sums = jax.ShapeDtypeStruct((n_xh, per_first + img_part, width), BF16)
    acts = jax.ShapeDtypeStruct((rows, w_in.shape[1]), F32)
    sent, pre_act = call(
        functools.partial(forward_kernel, per_first, img_part),
        (sums, acts),
        4 * rows * width * w_in.shape[1],
        here,
        captions,
        w_in,
        w_out,
        images,
        place=pltpu.HBM,
        grant=GRANT,
        scratch=[
            pltpu.VMEM(captions.shape, BF16),
            pltpu.VMEM(w_in.shape, BF16),
            pltpu.VMEM(w_out.shape, BF16),
            pltpu.VMEM((img_part, width), BF16),
            pltpu.VMEM(sums.shape, BF16),
            pltpu.VMEM(acts.shape, F32),
            pltpu.SemaphoreType.DMA((9,)),
        ],
    )
    got = exchange(sent, CHIPS, first)
    partial = jnp.sum(got[:, :per_first].astype(F32), axis=0).astype(BF16)
    img = got[:, per_first:].reshape(n_xh * img_part, width).astype(F32)
    img = (img * lax.rsqrt(jnp.sum(img * img, axis=1, keepdims=True) + EPS)).astype(BF16)
    sent = jnp.concatenate([partial.reshape(n_z, own, width), to_all(img, n_z)], axis=1)
    got = exchange(sent, CHIPS, second)
    embedding = jnp.sum(got[:, :own].astype(F32), axis=0)
    embedding, img = lax.optimization_barrier((embedding, got[:, own:].reshape(-1, width)))

    at_first, at_second = place(core, n_z, n_xh, lax.axis_index("z"), lax.axis_index("xh"))
    pair = lax.dynamic_slice_in_dim(pairs, at_first * per_first + at_second * own, own, 0)
    pair = jnp.broadcast_to(pair[:, None], (own, 128))
    row = jax.ShapeDtypeStruct((own, width), F32)
    unit_dir, inv_norm, unit = call(
        norm_kernel,
        (row, jax.ShapeDtypeStruct((own, 128), F32), jax.ShapeDtypeStruct((own, width + 128), BF16)),
        own * width,
        here,
        embedding,
        pair,
    )
    unit, img = lax.optimization_barrier((unit, img))
    other_img = lax.ppermute(img, "core", swap)
    other_unit = lax.ppermute(unit, "xl", swap)
    score = functools.partial(score_kernel, (n_z, n_xh, img_block, img_part))
    flops = 8 * own * img.shape[0] * width
    grad = call(score, row, flops, here, unit, img, other_img)
    other_grad = call(score, row, flops, here, other_unit, img, other_img)
    other_grad = lax.ppermute(other_grad, "xl", swap)
    sent = call(
        project_kernel,
        jax.ShapeDtypeStruct((n_z, own, width), BF16),
        own * width,
        here,
        unit_dir,
        inv_norm,
        grad,
        other_grad,
    )
    got = exchange(sent, CHIPS, second).reshape(per_first, width)
    embed_half = exchange(to_all(got, n_xh), CHIPS, first).reshape(rows, width)

    share = width // n_dp
    grads = (n_dp // n_core, 2 * share, w_in.shape[1])
    mine, other = call(
        functools.partial(backward_kernel, share),
        (jax.ShapeDtypeStruct(grads, F32), jax.ShapeDtypeStruct(grads, BF16)),
        6 * rows * width * w_in.shape[1],
        here,
        captions,
        embed_half,
        w_out,
        pre_act,
    )
    mine = mine + lax.ppermute(other, "core", swap).astype(F32)
    total = jnp.sum(exchange(mine.astype(BF16), ("y", "xl")).astype(F32), axis=0)
    return total[:share], total[share:]


def solution(mesh):
    fine = Mesh(mesh.devices.reshape(8, 2, 2, 8, 4), (*DP, *BLK))
    placed = (P(DP, None), P(None, BLK), P(BLK, None), P(BLK, None), P(DP))
    return jax.shard_map(
        body, mesh=fine, in_specs=placed, out_specs=(P(DP, BLK), P(DP, BLK)), check_vma=False
    )
```

```python
import functools
import math

import jax
import jax.numpy as jnp
from jax import lax
from jax.experimental import pallas as pl
from jax.experimental.pallas import tpu as pltpu
from jax.sharding import Mesh
from jax.sharding import PartitionSpec as P


DP = ("y", "xl", "core")
BLK = ("z", "xh")
CHIPS = ("core", "z", "xh")

SCALE = 10.0
BIAS = -5.0
EPS = 1e-06
DIGIT = 32
LANES = 128
CURVE = math.sqrt(2.0 / math.pi)
CUBIC = 0.044715
GRANT = 60 * 1024 * 1024
BF16 = jnp.bfloat16
F32 = jnp.float32


def exchange(x, axes, groups=None):
    return lax.all_to_all(x, axes, 0, 0, axis_index_groups=groups, tiled=True)


def to_all(x, n):
    return jnp.broadcast_to(x[None], (n, *x.shape))


def blk_groups(n_z, n_xh):
    zero = [[(z, xh) for z in range(n_z)] for xh in range(n_xh)]
    fine = n_z // n_xh
    one = [[(zh * fine + zl, xh) for zl in range(fine) for xh in range(n_xh)] for zh in range(n_xh)]
    grids = [[[core * n_z * n_xh + z * n_xh + xh for z, xh in row] for row in grid] for core, grid in enumerate((zero, one))]
    first = [list(column) for grid in grids for column in zip(*grid)]
    second = [row for grid in grids for row in grid]
    return first, second


def bend(v):
    return jnp.tanh(CURVE * (v + CUBIC * (v * v * v)))


def place(core, n_z, n_xh, z, xh):
    flat = z * n_xh + xh
    return jnp.where(core == 0, xh, flat // n_z), jnp.where(core == 0, z, flat % n_z)


def forward_kernel(
    per_first, img_part, where, captions_hbm, w_in_hbm, w_out_hbm, images_hbm, out_hbm, pre_hbm,
    captions_ref, w_in_ref, w_out_ref, img_ref, out_ref, pre_ref, sems
):
    n = out_ref.shape[0] // 2
    half = n * per_first
    start = pl.multiple_of(where[0] * img_part, img_part)
    fetch_in = pltpu.make_async_copy(w_in_hbm, w_in_ref, sems.at[0])
    fetch_out = pltpu.make_async_copy(w_out_hbm, w_out_ref, sems.at[1])
    fetch_img = pltpu.make_async_copy(images_hbm.at[pl.ds(start, img_part)], img_ref, sems.at[2])
    blocks = [pl.ds(k * half, half) for k in range(2)]
    fetches = [
        pltpu.make_async_copy(captions_hbm.at[at], captions_ref.at[at], sems.at[3 + k]) for k, at in enumerate(blocks)
    ]
    for copy in (fetch_in, fetches[0], fetch_out, fetch_img, fetches[1]):
        copy.start()
    stores = []
    fetch_in.wait()
    for k, at in enumerate(blocks):
        fetches[k].wait()
        pre_act = jnp.dot(captions_ref[at, :], w_in_ref[...], preferred_element_type=F32)
        pre_ref[at, :] = pre_act
        hidden = (0.5 * pre_act * (1.0 + bend(pre_act))).astype(BF16)
        if k == 0:
            fetch_out.wait()
            fetch_img.wait()
        total = jnp.dot(hidden, w_out_ref[...], preferred_element_type=F32).astype(BF16)
        for q in range(n):
            out_ref[k * n + q, :per_first] = total[q * per_first : (q + 1) * per_first]
            out_ref[k * n + q, per_first:] = img_ref[...]
        to = pl.ds(k * n, n)
        stores.append(pltpu.make_async_copy(out_ref.at[to], out_hbm.at[to], sems.at[5 + k]))
        stores.append(pltpu.make_async_copy(pre_ref.at[at], pre_hbm.at[at], sems.at[7 + k]))
        stores[-2].start()
        stores[-1].start()
    for copy in stores:
        copy.wait()


def backward_kernel(share, where, captions_ref, embed_ref, w_out_ref, pre_ref, mine_ref, other_ref):
    embed_half = embed_ref[...]
    hidden_grad = lax.dot_general(embed_half, w_out_ref[...], (((1,), (1,)), ((), ())), preferred_element_type=F32)
    v = pre_ref[...]
    t = bend(v)
    hidden = (0.5 * v * (1.0 + t)).astype(BF16)
    slope = 0.5 * (1.0 + t) + 0.5 * v * (1.0 - t * t) * (CURVE * (1.0 + 3.0 * CUBIC * v * v))
    preact_grad = (hidden_grad * slope).astype(BF16)
    over_rows = (((0,), (0,)), ((), ()))
    grad_in = lax.dot_general(preact_grad, captions_ref[...], over_rows, preferred_element_type=F32).T
    grad_out = lax.dot_general(hidden, embed_half, over_rows, preferred_element_type=F32).T
    zero = where[0] % 2 == 0
    for at, grad in ((0, grad_in), (share, grad_out)):
        for q in range(mine_ref.shape[0]):
            even = grad[2 * q * share : (2 * q + 1) * share]
            odd = grad[(2 * q + 1) * share : (2 * q + 2) * share]
            mine_ref[q, at : at + share] = jnp.where(zero, even, odd)
            other_ref[q, at : at + share] = jnp.where(zero, odd, even).astype(BF16)


def half_grad(spot, geometry, unit_half, pair, img):
    n_z, n_xh, img_block, img_part = geometry
    n = lax.broadcasted_iota(jnp.int32, (1, img.shape[0]), 1)
    slot, row = n // img_part, n % img_part
    block = jnp.where(spot % 2 == 0, slot, (slot % n_xh) * n_z + slot // n_xh)
    logits = SCALE * lax.dot_general(unit_half, img, (((1,), (1,)), ((), ())), preferred_element_type=F32) + BIAS
    column = block * img_block + spot * img_part + row
    mismatch = (jax.nn.sigmoid(logits) - (pair == column).astype(F32)).astype(BF16)
    return jnp.dot(mismatch, img, preferred_element_type=F32)


def norm_kernel(first, sum_ref, pairs_ref, dir_ref, norm_ref, unit_ref):
    embedding = sum_ref[...]
    own, width = embedding.shape
    inv_norm = lax.rsqrt(jnp.sum(embedding * embedding, axis=1, keepdims=True) + EPS)
    unit_dir = embedding * inv_norm
    dir_ref[...] = unit_dir
    norm_ref[...] = jnp.broadcast_to(inv_norm, norm_ref.shape)
    lane = lax.broadcasted_iota(jnp.int32, (own, LANES), 1)
    spot = first[0] % LANES + lax.broadcasted_iota(jnp.int32, (own, LANES), 0)
    line = jnp.broadcast_to(pairs_ref[pl.ds(first[0] // LANES, 1), :], (own, LANES))
    pair = jnp.sum(jnp.where(lane == spot, line, 0).astype(F32), axis=1, keepdims=True).astype(jnp.int32)
    digits = jnp.where(lane == 0, pair // DIGIT, jnp.where(lane == 1, pair % DIGIT, 0))
    unit_ref[:, :width] = unit_dir.astype(BF16)
    unit_ref[:, width:] = digits.astype(F32).astype(BF16)


def score_kernel(geometry, where, unit_ref, mine_ref, other_ref, grad_ref):
    width = grad_ref.shape[1]
    spot = where[0]
    digits = unit_ref[:, width:].astype(F32)
    pair = (digits[:, :1] * DIGIT + digits[:, 1:2]).astype(jnp.int32)
    unit_half = unit_ref[:, :width]
    grad_ref[...] = half_grad(spot, geometry, unit_half, pair, mine_ref[...]) + half_grad(
        spot + 1 - 2 * (spot % 2), geometry, unit_half, pair, other_ref[...]
    )


def project_kernel(where, dir_ref, norm_ref, mine_ref, other_ref, out_ref):
    unit_dir = dir_ref[...]
    unit_grad = SCALE * (mine_ref[...] + other_ref[...])
    along = jnp.sum(unit_dir * unit_grad, axis=1, keepdims=True)
    embed_half = ((unit_grad - unit_dir * along) * norm_ref[:, :1]).astype(BF16)
    for k in range(out_ref.shape[0]):
        out_ref[k] = embed_half


def call(kernel, outs, flops, *args, place=pltpu.VMEM, scratch=(), grant=16 * 1024 * 1024):
    whole = pl.BlockSpec(memory_space=place)
    return pl.pallas_call(
        kernel,
        out_shape=outs,
        in_specs=[pl.BlockSpec(memory_space=pltpu.SMEM)] + [whole] * (len(args) - 1),
        out_specs=jax.tree.map(lambda _: whole, outs),
        scratch_shapes=scratch,
        compiler_params=pltpu.CompilerParams(vmem_limit_bytes=grant),
        cost_estimate=pl.CostEstimate(flops=flops, bytes_accessed=3_000_000, transcendentals=0),
    )(*args)


def body(captions, w_in, w_out, images, pairs):
    rows, width = captions.shape
    n_z, n_xh, n_dp = lax.axis_size("z"), lax.axis_size("xh"), lax.axis_size(DP)
    n_core = lax.axis_size("core")
    core = lax.axis_index("core")
    swap = [(i, n_core - 1 - i) for i in range(n_core)]
    first, second = blk_groups(n_z, n_xh)
    per_first = rows // n_xh
    own = per_first // n_z
    img_block = images.shape[0]
    img_part = img_block // (n_core * lax.axis_size("xl"))

    here = lax.axis_index(("xl", "core")).reshape(1).astype(jnp.int32)
    sums = jax.ShapeDtypeStruct((n_xh, per_first + img_part, width), BF16)
    acts = jax.ShapeDtypeStruct((rows, w_in.shape[1]), F32)
    sent, pre_act = call(
        functools.partial(forward_kernel, per_first, img_part),
        (sums, acts),
        4 * rows * width * w_in.shape[1],
        here,
        captions,
        w_in,
        w_out,
        images,
        place=pltpu.HBM,
        grant=GRANT,
        scratch=[
            pltpu.VMEM(captions.shape, BF16),
            pltpu.VMEM(w_in.shape, BF16),
            pltpu.VMEM(w_out.shape, BF16),
            pltpu.VMEM((img_part, width), BF16),
            pltpu.VMEM(sums.shape, BF16),
            pltpu.VMEM(acts.shape, F32),
            pltpu.SemaphoreType.DMA((9,)),
        ],
    )
    got = exchange(sent, CHIPS, first)
    partial = jnp.sum(got[:, :per_first].astype(F32), axis=0).astype(BF16)
    img = got[:, per_first:].reshape(n_xh * img_part, width).astype(F32)
    img = (img * lax.rsqrt(jnp.sum(img * img, axis=1, keepdims=True) + EPS)).astype(BF16)
    sent = jnp.concatenate([partial.reshape(n_z, own, width), to_all(img, n_z)], axis=1)
    at_first, at_second = place(core, n_z, n_xh, lax.axis_index("z"), lax.axis_index("xh"))
    begin = (at_first * per_first + at_second * own).reshape(1).astype(jnp.int32)
    sent, begin = lax.optimization_barrier((sent, begin))
    got = exchange(sent, CHIPS, second)
    embedding = jnp.sum(got[:, :own].astype(F32), axis=0)
    embedding, img = lax.optimization_barrier((embedding, got[:, own:].reshape(-1, width)))

    row = jax.ShapeDtypeStruct((own, width), F32)
    unit_dir, inv_norm, unit = call(
        norm_kernel,
        (row, jax.ShapeDtypeStruct((own, LANES), F32), jax.ShapeDtypeStruct((own, width + LANES), BF16)),
        own * width,
        begin,
        embedding,
        pairs.reshape(-1, LANES),
    )
    unit, img = lax.optimization_barrier((unit, img))
    other_unit = lax.ppermute(unit, "xl", swap)
    other_img = lax.ppermute(img, "core", swap)
    score = functools.partial(score_kernel, (n_z, n_xh, img_block, img_part))
    flops = 8 * own * img.shape[0] * width
    grad = call(score, row, flops, here, unit, img, other_img)
    other_grad = call(score, row, flops, here, other_unit, img, other_img)
    other_grad = lax.ppermute(other_grad, "xl", swap)
    sent = call(
        project_kernel,
        jax.ShapeDtypeStruct((n_z, own, width), BF16),
        own * width,
        here,
        unit_dir,
        inv_norm,
        grad,
        other_grad,
    )
    got = exchange(sent, CHIPS, second).reshape(per_first, width)
    embed_half = exchange(to_all(got, n_xh), CHIPS, first).reshape(rows, width)

    share = width // n_dp
    grads = (n_dp // n_core, 2 * share, w_in.shape[1])
    mine, other = call(
        functools.partial(backward_kernel, share),
        (jax.ShapeDtypeStruct(grads, F32), jax.ShapeDtypeStruct(grads, BF16)),
        6 * rows * width * w_in.shape[1],
        here,
        captions,
        embed_half,
        w_out,
        pre_act,
    )
    mine = mine + lax.ppermute(other, "core", swap).astype(F32)
    total = jnp.sum(exchange(mine.astype(BF16), ("y", "xl")).astype(F32), axis=0)
    return total[:share], total[share:]


def solution(mesh):
    fine = Mesh(mesh.devices.reshape(8, 2, 2, 8, 4), (*DP, *BLK))
    placed = (P(DP, None), P(None, BLK), P(BLK, None), P(BLK, None), P(DP))
    return jax.shard_map(
        body, mesh=fine, in_specs=placed, out_specs=(P(DP, BLK), P(DP, BLK)), check_vma=False
    )
```

```python
import functools
import math

import jax
import jax.numpy as jnp
from jax import lax
from jax.experimental import pallas as pl
from jax.experimental.pallas import tpu as pltpu
from jax.sharding import Mesh
from jax.sharding import PartitionSpec as P


DP = ("y", "xl", "core")
BLK = ("z", "xh")
CHIPS = ("core", "z", "xh")

SCALE = 10.0
BIAS = -5.0
EPS = 1e-06
DIGIT = 32
LANES = 128
CURVE = math.sqrt(2.0 / math.pi)
CUBIC = 0.044715
GRANT = 60 * 1024 * 1024
BF16 = jnp.bfloat16
F32 = jnp.float32


def exchange(x, axes, groups=None):
    return lax.all_to_all(x, axes, 0, 0, axis_index_groups=groups, tiled=True)


def to_all(x, n):
    return jnp.broadcast_to(x[None], (n, *x.shape))


def blk_groups(n_z, n_xh):
    zero = [[(z, xh) for z in range(n_z)] for xh in range(n_xh)]
    fine = n_z // n_xh
    one = [[(zh * fine + zl, xh) for zl in range(fine) for xh in range(n_xh)] for zh in range(n_xh)]
    grids = [[[core * n_z * n_xh + z * n_xh + xh for z, xh in row] for row in grid] for core, grid in enumerate((zero, one))]
    first = [list(column) for grid in grids for column in zip(*grid)]
    second = [row for grid in grids for row in grid]
    return first, second


def bend(v):
    return jnp.tanh(CURVE * (v + CUBIC * (v * v * v)))


def place(core, n_z, n_xh, z, xh):
    flat = z * n_xh + xh
    return jnp.where(core == 0, xh, flat // n_z), jnp.where(core == 0, z, flat % n_z)


def forward_kernel(
    per_first, img_part, where, captions_hbm, w_in_hbm, w_out_hbm, images_hbm, out_hbm, pre_hbm,
    captions_ref, w_in_ref, w_out_ref, img_ref, out_ref, pre_ref, sems
):
    n = out_ref.shape[0] // 2
    half = n * per_first
    start = pl.multiple_of(where[0] * img_part, img_part)
    fetch_in = pltpu.make_async_copy(w_in_hbm, w_in_ref, sems.at[0])
    fetch_out = pltpu.make_async_copy(w_out_hbm, w_out_ref, sems.at[1])
    fetch_img = pltpu.make_async_copy(images_hbm.at[pl.ds(start, img_part)], img_ref, sems.at[2])
    blocks = [pl.ds(k * half, half) for k in range(2)]
    fetches = [
        pltpu.make_async_copy(captions_hbm.at[at], captions_ref.at[at], sems.at[3 + k]) for k, at in enumerate(blocks)
    ]
    for copy in (fetch_img, fetch_in, fetches[0], fetch_out, fetches[1]):
        copy.start()
    stores = []
    fetch_img.wait()
    img = img_ref[...].astype(F32)
    img = (img * lax.rsqrt(jnp.sum(img * img, axis=1, keepdims=True) + EPS)).astype(BF16)
    fetch_in.wait()
    for k, at in enumerate(blocks):
        fetches[k].wait()
        pre_act = jnp.dot(captions_ref[at, :], w_in_ref[...], preferred_element_type=F32)
        pre_ref[at, :] = pre_act
        hidden = (0.5 * pre_act * (1.0 + bend(pre_act))).astype(BF16)
        if k == 0:
            fetch_out.wait()
        total = jnp.dot(hidden, w_out_ref[...], preferred_element_type=F32).astype(BF16)
        for q in range(n):
            out_ref[k * n + q, :per_first] = total[q * per_first : (q + 1) * per_first]
            out_ref[k * n + q, per_first:] = img
        to = pl.ds(k * n, n)
        stores.append(pltpu.make_async_copy(out_ref.at[to], out_hbm.at[to], sems.at[5 + k]))
        stores.append(pltpu.make_async_copy(pre_ref.at[at], pre_hbm.at[at], sems.at[7 + k]))
        stores[-2].start()
        stores[-1].start()
    for copy in stores:
        copy.wait()


def backward_kernel(share, where, captions_ref, embed_ref, w_out_ref, pre_ref, mine_ref, other_ref):
    embed_half = embed_ref[...]
    hidden_grad = lax.dot_general(embed_half, w_out_ref[...], (((1,), (1,)), ((), ())), preferred_element_type=F32)
    v = pre_ref[...]
    t = bend(v)
    hidden = (0.5 * v * (1.0 + t)).astype(BF16)
    slope = 0.5 * (1.0 + t) + 0.5 * v * (1.0 - t * t) * (CURVE * (1.0 + 3.0 * CUBIC * v * v))
    preact_grad = (hidden_grad * slope).astype(BF16)
    over_rows = (((0,), (0,)), ((), ()))
    grad_in = lax.dot_general(preact_grad, captions_ref[...], over_rows, preferred_element_type=F32).T
    grad_out = lax.dot_general(hidden, embed_half, over_rows, preferred_element_type=F32).T
    zero = where[0] % 2 == 0
    for at, grad in ((0, grad_in), (share, grad_out)):
        for q in range(mine_ref.shape[0]):
            even = grad[2 * q * share : (2 * q + 1) * share]
            odd = grad[(2 * q + 1) * share : (2 * q + 2) * share]
            mine_ref[q, at : at + share] = jnp.where(zero, even, odd)
            other_ref[q, at : at + share] = jnp.where(zero, odd, even).astype(BF16)


def half_grad(spot, geometry, unit_half, pair, img):
    n_z, n_xh, img_block, img_part = geometry
    n = lax.broadcasted_iota(jnp.int32, (1, img.shape[0]), 1)
    slot, row = n // img_part, n % img_part
    block = jnp.where(spot % 2 == 0, slot, (slot % n_xh) * n_z + slot // n_xh)
    logits = SCALE * lax.dot_general(unit_half, img, (((1,), (1,)), ((), ())), preferred_element_type=F32) + BIAS
    column = block * img_block + spot * img_part + row
    mismatch = (jax.nn.sigmoid(logits) - (pair == column).astype(F32)).astype(BF16)
    return jnp.dot(mismatch, img, preferred_element_type=F32)


def norm_kernel(first, sum_ref, pairs_ref, dir_ref, norm_ref, unit_ref):
    embedding = sum_ref[...]
    own, width = embedding.shape
    inv_norm = lax.rsqrt(jnp.sum(embedding * embedding, axis=1, keepdims=True) + EPS)
    unit_dir = embedding * inv_norm
    dir_ref[...] = unit_dir
    norm_ref[...] = jnp.broadcast_to(inv_norm, norm_ref.shape)
    lane = lax.broadcasted_iota(jnp.int32, (own, LANES), 1)
    spot = first[0] % LANES + lax.broadcasted_iota(jnp.int32, (own, LANES), 0)
    line = jnp.broadcast_to(pairs_ref[pl.ds(first[0] // LANES, 1), :], (own, LANES))
    pair = jnp.sum(jnp.where(lane == spot, line, 0).astype(F32), axis=1, keepdims=True).astype(jnp.int32)
    digits = jnp.where(lane == 0, pair // DIGIT, jnp.where(lane == 1, pair % DIGIT, 0))
    unit_ref[:, :width] = unit_dir.astype(BF16)
    unit_ref[:, width:] = digits.astype(F32).astype(BF16)


def score_kernel(geometry, where, unit_ref, mine_ref, other_ref, grad_ref):
    width = grad_ref.shape[1]
    spot = where[0]
    digits = unit_ref[:, width:].astype(F32)
    pair = (digits[:, :1] * DIGIT + digits[:, 1:2]).astype(jnp.int32)
    unit_half = unit_ref[:, :width]
    grad_ref[...] = half_grad(spot, geometry, unit_half, pair, mine_ref[...]) + half_grad(
        spot + 1 - 2 * (spot % 2), geometry, unit_half, pair, other_ref[...]
    )


def project_kernel(where, dir_ref, norm_ref, mine_ref, other_ref, out_ref):
    unit_dir = dir_ref[...]
    unit_grad = SCALE * (mine_ref[...] + other_ref[...])
    along = jnp.sum(unit_dir * unit_grad, axis=1, keepdims=True)
    embed_half = ((unit_grad - unit_dir * along) * norm_ref[:, :1]).astype(BF16)
    for k in range(out_ref.shape[0]):
        out_ref[k] = embed_half


def call(kernel, outs, flops, *args, place=pltpu.VMEM, scratch=(), grant=16 * 1024 * 1024):
    whole = pl.BlockSpec(memory_space=place)
    return pl.pallas_call(
        kernel,
        out_shape=outs,
        in_specs=[pl.BlockSpec(memory_space=pltpu.SMEM)] + [whole] * (len(args) - 1),
        out_specs=jax.tree.map(lambda _: whole, outs),
        scratch_shapes=scratch,
        compiler_params=pltpu.CompilerParams(vmem_limit_bytes=grant),
        cost_estimate=pl.CostEstimate(flops=flops, bytes_accessed=3_000_000, transcendentals=0),
    )(*args)


def body(captions, w_in, w_out, images, pairs):
    rows, width = captions.shape
    n_z, n_xh, n_dp = lax.axis_size("z"), lax.axis_size("xh"), lax.axis_size(DP)
    n_core = lax.axis_size("core")
    core = lax.axis_index("core")
    swap = [(i, n_core - 1 - i) for i in range(n_core)]
    first, second = blk_groups(n_z, n_xh)
    per_first = rows // n_xh
    own = per_first // n_z
    img_block = images.shape[0]
    img_part = img_block // (n_core * lax.axis_size("xl"))

    here = lax.axis_index(("xl", "core")).reshape(1).astype(jnp.int32)
    sums = jax.ShapeDtypeStruct((n_xh, per_first + img_part, width), BF16)
    acts = jax.ShapeDtypeStruct((rows, w_in.shape[1]), F32)
    sent, pre_act = call(
        functools.partial(forward_kernel, per_first, img_part),
        (sums, acts),
        4 * rows * width * w_in.shape[1],
        here,
        captions,
        w_in,
        w_out,
        images,
        place=pltpu.HBM,
        grant=GRANT,
        scratch=[
            pltpu.VMEM(captions.shape, BF16),
            pltpu.VMEM(w_in.shape, BF16),
            pltpu.VMEM(w_out.shape, BF16),
            pltpu.VMEM((img_part, width), BF16),
            pltpu.VMEM(sums.shape, BF16),
            pltpu.VMEM(acts.shape, F32),
            pltpu.SemaphoreType.DMA((9,)),
        ],
    )
    got = exchange(sent, CHIPS, first)
    partial = jnp.sum(got[:, :per_first].astype(F32), axis=0).astype(BF16)
    img = got[:, per_first:].reshape(n_xh * img_part, width)
    sent = jnp.concatenate([partial.reshape(n_z, own, width), to_all(img, n_z)], axis=1)
    at_first, at_second = place(core, n_z, n_xh, lax.axis_index("z"), lax.axis_index("xh"))
    begin = (at_first * per_first + at_second * own).reshape(1).astype(jnp.int32)
    sent, begin = lax.optimization_barrier((sent, begin))
    got = exchange(sent, CHIPS, second)
    embedding = jnp.sum(got[:, :own].astype(F32), axis=0)
    embedding, img = lax.optimization_barrier((embedding, got[:, own:].reshape(-1, width)))

    row = jax.ShapeDtypeStruct((own, width), F32)
    unit_dir, inv_norm, unit = call(
        norm_kernel,
        (row, jax.ShapeDtypeStruct((own, LANES), F32), jax.ShapeDtypeStruct((own, width + LANES), BF16)),
        own * width,
        begin,
        embedding,
        pairs.reshape(-1, LANES),
    )
    unit, img = lax.optimization_barrier((unit, img))
    other_unit = lax.ppermute(unit, "xl", swap)
    other_img = lax.ppermute(img, "core", swap)
    score = functools.partial(score_kernel, (n_z, n_xh, img_block, img_part))
    flops = 8 * own * img.shape[0] * width
    grad = call(score, row, flops, here, unit, img, other_img)
    other_grad = call(score, row, flops, here, other_unit, img, other_img)
    other_grad = lax.ppermute(other_grad, "xl", swap)
    sent = call(
        project_kernel,
        jax.ShapeDtypeStruct((n_z, own, width), BF16),
        own * width,
        here,
        unit_dir,
        inv_norm,
        grad,
        other_grad,
    )
    got = exchange(sent, CHIPS, second).reshape(per_first, width)
    embed_half = exchange(to_all(got, n_xh), CHIPS, first).reshape(rows, width)

    share = width // n_dp
    grads = (n_dp // n_core, 2 * share, w_in.shape[1])
    mine, other = call(
        functools.partial(backward_kernel, share),
        (jax.ShapeDtypeStruct(grads, F32), jax.ShapeDtypeStruct(grads, BF16)),
        6 * rows * width * w_in.shape[1],
        here,
        captions,
        embed_half,
        w_out,
        pre_act,
    )
    mine = mine + lax.ppermute(other, "core", swap).astype(F32)
    total = jnp.sum(exchange(mine.astype(BF16), ("y", "xl")).astype(F32), axis=0)
    return total[:share], total[share:]


def solution(mesh):
    fine = Mesh(mesh.devices.reshape(8, 2, 2, 8, 4), (*DP, *BLK))
    placed = (P(DP, None), P(None, BLK), P(BLK, None), P(BLK, None), P(DP))
    return jax.shard_map(
        body, mesh=fine, in_specs=placed, out_specs=(P(DP, BLK), P(DP, BLK)), check_vma=False
    )
```
